1024 devices in a mesh: out: 32 (over z), con: 16 (over y, x_hi, core), occ: 2 (over x_lo).
Axes of the slice: x: 4 (x_hi: 2, x_lo: 2; x = x_hi * 2 + x_lo), y: 4, z: 32, core: 2. Of those that a mesh axis runs over, the one named last changes fastest.
Arguments:
- amplitudes: float32 [2048, 64, 64], P('con', 'occ', 'out'), may hold values from -6 to 6
- fit_out: float32 [1024, 8192], P('con', 'out'), may hold values from -0.12 to 0.12
- fit_con: float32 [1024, 2048], P(None, 'con'), may hold values from -0.12 to 0.12
- hole_hole: float32 [64, 64], replicated, may hold values from -0.75 to 0.75
Outputs:
- ladder: float32 [8192, 64, 64], P(('out', 'con'), 'occ')
The draws below stay inside these ranges and needn't reach their ends.
All inputs are finite; a program needn't handle non-finite values.
Results may differ from the reference program's by a relative error of at most 0.000075.
Values sent between devices are 32-bit elements; how exact they have to be, the bound alone decides.
No kernel may reach another device: no remote copies, remote signals or barrier semaphores. Data moves between devices by JAX's collectives and lax.ppermute only.
A program may use at most 32 MiB of HBM per device.

```python
import jax
import jax.numpy as jnp
from jax import lax

NOCC = 64
NAUX = 1024
NP = 8192
NQ = 2048


def steps_of(rng, shape, split, smallest, top_value):
    gain = 1.0
    for dim, shards_of in split:
        steps = jax.random.uniform(jax.random.fold_in(jax.random.fold_in(rng, 6), dim), (shards_of,), jnp.float32, smallest / len(split), top_value / len(split))
        gain = gain * jnp.repeat(jnp.exp(steps), shape[dim] // shards_of).reshape((-1,) + (1,) * (len(shape) - 1 - dim))
    return gain


def normal_values(stream_key, extent, spread, bound, pieces=(), kind=jnp.bfloat16):
    result = jax.random.normal(stream_key, extent, jnp.float32) * spread
    if len(pieces) > 0:
        result = steps_of(stream_key, extent, pieces, -0.22, 0.18) * result
    return jnp.clip(result, min=-bound, max=bound).astype(kind)


def setup_inputs(seed: int = 0) -> dict:
    splits = jax.random.split(jax.random.key(seed), 5)
    return {
        "amplitudes": normal_values(splits[0], (NQ, NOCC, NOCC), 1.0, 6.0, ((0, 16), (1, 2), (2, 32)), jnp.float32),
        "fit_out": normal_values(splits[1], (NAUX, NP), 0.02, 0.12, ((0, 16), (1, 32)), jnp.float32),
        "fit_con": normal_values(splits[2], (NAUX, NQ), 0.02, 0.12, ((1, 16),), jnp.float32),
        "hole_hole": normal_values(splits[3], (NOCC, NOCC), NOCC ** -0.5, 0.75, (), jnp.float32),
    }


def reference(amplitudes, fit_out, fit_con, hole_hole):
    highest = lax.Precision.HIGHEST
    dress = jnp.eye(hole_hole.shape[0], dtype=jnp.float32) - hole_hole
    tile = jnp.dot(fit_out.T, fit_con, precision=highest)
    half = jnp.einsum("qim,jm->qij", amplitudes, dress, precision=highest)
    dressed = jnp.einsum("im,qmj->qij", dress, half, precision=highest)
    flat = dressed.reshape(dressed.shape[0], -1)
    ladder = jnp.dot(tile, flat, precision=highest)
    return ladder.reshape(tile.shape[0], dressed.shape[1], dressed.shape[2])
```

```python
import jax
import jax.numpy as jnp
from jax import lax
from jax.sharding import PartitionSpec as P

highest = lax.Precision.HIGHEST


def copy_for_each(array, axis, groups=None):
    length = lax.axis_size(axis) if groups is None else len(groups[0])
    return lax.all_to_all(
        jnp.broadcast_to(array[None], (length, *array.shape)),
        axis, 0, 0, tiled=True, axis_index_groups=groups,
    )


def local(amplitudes, fit_out, fit_con, hole_hole):
    norbs = hole_hole.shape[0]
    outs, cons, occs = lax.axis_size("out"), lax.axis_size("con"), lax.axis_size("occ")
    plane = cons * occs
    naux = fit_con.shape[0]
    own = amplitudes.shape[1]
    cols = amplitudes.shape[2]
    kept = norbs // plane
    dress = jnp.eye(norbs, dtype=jnp.float32) - hole_hole

    first = lax.axis_index("occ") * own
    columns = lax.dynamic_slice_in_dim(dress, first, own, 1)
    half = jnp.einsum("im,qmj->ijq", columns, amplitudes, precision=highest)
    half = half.reshape(-1, half.shape[2])
    share = jnp.einsum("pq,lq->pl", half, fit_con, precision=highest)
    share = share.reshape(occs, cons, kept * cols, naux)
    share = jnp.swapaxes(share, 0, 1).reshape(plane, kept * cols, naux)
    parts = lax.all_to_all(share, ("con", "occ"), 0, 0, tiled=True)
    fitted = jnp.sum(parts, axis=0)
    parity = [[2 * k + r for k in range(outs // 2)] for r in range(2)]
    pairs = [[2 * k + r for r in range(2)] for k in range(outs // 2)]
    strided = lax.all_gather(fitted, "out", axis=0, axis_index_groups=parity)
    whole = copy_for_each(strided, "out", pairs)
    factors = copy_for_each(fit_out, "con")
    factors = factors.reshape(naux, -1)
    ladder = jnp.einsum("pl,la->pa", whole.reshape(kept * norbs, naux), factors, precision=highest)
    orders = dress.T.reshape(outs // 2, 2, cols, norbs)
    orders = jnp.swapaxes(orders, 0, 1)
    blocks = jnp.einsum("ik,zhjn->zhkjin", jnp.eye(kept, dtype=jnp.float32), orders, precision=highest)
    blocks = blocks.reshape(kept * norbs, kept * norbs)
    ladder = jnp.einsum("pa,pn->an", ladder, blocks, precision=highest)
    rows = ladder.shape[0] // cons
    ladder = ladder.reshape(cons, rows, kept * norbs)
    ladder = lax.all_to_all(ladder, "con", 0, 0, tiled=True)
    ladder = ladder.reshape(cons, rows, kept, norbs)
    return jnp.swapaxes(ladder, 0, 1).reshape(rows, cons * kept, norbs)


def solution(mesh):
    placed = (P("con", "occ", "out"), P("con", "out"), P(None, "con"), P())
    return jax.shard_map(
        local, mesh=mesh, in_specs=placed, out_specs=P(("out", "con"), "occ", None), check_vma=False
    )
```

```python
import jax
import jax.numpy as jnp
from jax import lax
from jax.experimental import pallas as pl
from jax.experimental.pallas import tpu as pltpu
from jax.sharding import Mesh, PartitionSpec as P

highest = lax.Precision.HIGHEST
plane = ("con", "occ")
pair = ("out_lo", "con")
lanes = 128
room = 16 * 1024 * 1024


def dot(a, b):
    return jnp.dot(a, b, precision=highest, preferred_element_type=jnp.float32)


def contract_kernel(fitted_ref, factors_ref, ladder_ref):
    total = dot(fitted_ref[...], factors_ref[...])
    blocks, rows, _ = ladder_ref.shape
    turned = total.T.reshape(blocks, 2, rows, total.shape[0])
    ladder_ref[...] = jnp.concatenate([turned[:, 0], turned[:, 1]], axis=-1)


def contract(fitted, factors, blocks):
    cols, pairs = fitted.shape[0], factors.shape[1]
    return pl.pallas_call(
        contract_kernel,
        out_shape=jax.ShapeDtypeStruct((blocks, pairs // blocks // 2, 2 * cols), jnp.float32),
        in_specs=[pl.BlockSpec(memory_space=pltpu.VMEM)] * 2,
        out_specs=pl.BlockSpec(memory_space=pltpu.VMEM),
        compiler_params=pltpu.CompilerParams(vmem_limit_bytes=room),
    )(fitted, factors)


def finish_kernel(ladder_ref, blocks_ref, out_ref, held):
    lots = blocks_ref.shape[0]
    total = None
    for z in range(lots):
        term = dot(ladder_ref[z], blocks_ref[z])
        total = term if z == 0 else total + term
    halves, kept, norbs = 2, held.shape[0] // 2, out_ref.shape[2]
    rows, cons = out_ref.shape[0] // halves, out_ref.shape[1] // kept
    for s in range(halves * kept):
        held[s] = total[:, s * lanes : (s + 1) * lanes]
    for h in range(halves):
        for i in range(kept):
            for r in range(rows):
                line = held[h * kept + i, pl.ds(r, cons, stride=rows), :]
                out_ref[h * rows + r, pl.ds(i, cons, stride=kept), :] = line[:, :norbs]


def finish(ladder, blocks, shape, kept):
    return pl.pallas_call(
        finish_kernel,
        out_shape=jax.ShapeDtypeStruct(shape, jnp.float32),
        in_specs=[pl.BlockSpec(memory_space=pltpu.VMEM)] * 2,
        out_specs=pl.BlockSpec(memory_space=pltpu.VMEM),
        scratch_shapes=[pltpu.VMEM((2 * kept, ladder.shape[1], lanes), jnp.float32)],
        compiler_params=pltpu.CompilerParams(vmem_limit_bytes=room),
    )(ladder, blocks)


def local(amplitudes, fit_out, fit_con, hole_hole):
    norbs = hole_hole.shape[0]
    naux = fit_con.shape[0]
    halves, lots = lax.axis_size("out_hi"), lax.axis_size("out_lo")
    cons, occs = lax.axis_size("con"), lax.axis_size("occ")
    own, cols = amplitudes.shape[1], amplitudes.shape[2]
    kept = norbs // (cons * occs)
    side = lax.axis_index("out_lo")
    dress = jnp.eye(norbs, dtype=jnp.float32) - hole_hole

    first = lax.axis_index("occ") * own
    columns = lax.dynamic_slice_in_dim(dress, first, own, 1)
    columns = jnp.swapaxes(columns.reshape(occs, cons, kept, own), 0, 1).reshape(norbs, own)
    half = jnp.einsum("im,qmj->ijq", columns, amplitudes, precision=highest)
    half = half.reshape(norbs * cols, half.shape[2])
    share = jnp.einsum("pq,lq->pl", half, fit_con, precision=highest)
    share = share.reshape(cons * occs, kept * cols, naux)
    parts = lax.all_to_all(share, plane, 0, 0, tiled=True)
    fitted = jnp.sum(parts, axis=0)
    whole = lax.all_gather(fitted, "out_hi", axis=0)
    whole = whole.reshape(halves * kept * cols, naux)
    other = lax.ppermute(fit_out, "out_lo", [(0, 1), (1, 0)])
    factors = jnp.concatenate(
        [jnp.where(side == 0, fit_out, other), jnp.where(side == 0, other, fit_out)], axis=1
    )
    factors = jnp.broadcast_to(factors[None], (cons, *factors.shape))
    factors = lax.all_to_all(factors, "con", 0, 0, tiled=True)
    factors = factors.reshape(naux, lots * fit_out.shape[1])
    ladder = contract(whole, factors, lots * cons)
    ladder = lax.all_to_all(ladder, pair, 0, 0, tiled=True)
    rows = fit_out.shape[1] // cons
    ladder = ladder.reshape(lots, cons * rows // 2, lanes)
    orders = jnp.swapaxes(dress.T.reshape(halves, lots, cols, norbs), 0, 1)
    orders = jnp.pad(orders, ((0, 0), (0, 0), (0, 0), (0, lanes - norbs)))
    orders = orders.reshape(lots, 1, halves, 1, cols, 1, 1, lanes)
    same = jnp.eye(2, dtype=jnp.float32).reshape(1, 2, 1, 1, 1, 2, 1, 1)
    kind = jnp.eye(kept, dtype=jnp.float32).reshape(1, 1, 1, kept, 1, 1, kept, 1)
    blocks = (orders * same * kind).reshape(lots, lanes, 2 * kept * lanes)
    return finish(ladder, blocks, (rows, cons * kept, norbs), kept)


def solution(mesh):
    lots = 2
    shape = dict(mesh.shape)
    devices = mesh.devices.reshape(shape["out"] // lots, lots, shape["con"], shape["occ"])
    finer = Mesh(devices, ("out_hi", "out_lo", "con", "occ"))
    out = ("out_hi", "out_lo")
    return jax.shard_map(
        local,
        mesh=finer,
        in_specs=(P("con", "occ", out), P("con", out), P(None, "con"), P()),
        out_specs=P((*out, "con"), "occ", None),
        check_vma=False,
    )
```

```python
import jax
import jax.numpy as jnp
from jax import lax
from jax.experimental import pallas as pl
from jax.experimental.pallas import tpu as pltpu
from jax.sharding import Mesh, PartitionSpec as P

highest = lax.Precision.HIGHEST
plane = ("con", "occ")
pair = ("out_lo", "con")
lanes = 128
room = 16 * 1024 * 1024


def dot(a, b):
    return jnp.dot(a, b, precision=highest, preferred_element_type=jnp.float32)


def parted(a):
    high = a.astype(jnp.bfloat16)
    rest = a - high.astype(jnp.float32)
    middle = rest.astype(jnp.bfloat16)
    return high, middle, (rest - middle.astype(jnp.float32)).astype(jnp.bfloat16)


def narrow(a, b, across):
    return lax.dot_general(a, b, (((1,), (across,)), ((), ())), preferred_element_type=jnp.float32)


def thin_dot(a, parts, across):
    high, middle, low = parts
    rows = a[0].shape[0]
    first = narrow(jnp.concatenate(a, axis=0), high, across)
    second = narrow(jnp.concatenate(a[:2], axis=0), middle, across)
    third = narrow(a[0], low, across)
    small = first[2 * rows :] + second[rows:] + third
    return first[:rows] + (first[rows : 2 * rows] + second[:rows] + small)


def lower_rows(shape):
    return lax.broadcasted_iota(jnp.int32, shape, len(shape) - 2) < shape[-2] // 2


def share_kernel(given_ref, lined_ref, hole_ref, share_ref, given, lined, hole, padded, arrived):
    own, cols, _ = given.shape
    norbs = hole.shape[0]
    blocks = 2 * share_ref.shape[0]
    occs = norbs // own
    kept = norbs // blocks
    half = lined.shape[0] // 2
    copies = [
        pltpu.make_async_copy(given_ref, given, arrived.at[0]),
        pltpu.make_async_copy(hole_ref, hole, arrived.at[1]),
    ]
    for c in range(2):
        rows = pl.ds(c * half, half)
        copies.append(pltpu.make_async_copy(lined_ref.at[rows, :], lined.at[rows, :], arrived.at[2 + c]))
    for copy in copies:
        copy.start()
    padded[...] = jnp.zeros_like(padded)
    place = lax.broadcasted_iota(jnp.int32, (blocks * cols * kept, norbs), 0)
    device, inner = place // (cols * kept), place % (cols * kept)
    wanted = (device % occs) * own + (device // occs) * kept + inner % kept
    index = lax.broadcasted_iota(jnp.int32, (blocks * cols * kept, norbs), 1)
    square = (norbs, norbs)
    unit = lax.broadcasted_iota(jnp.int32, square, 0) == lax.broadcasted_iota(jnp.int32, square, 1)
    first = pl.multiple_of(lax.axis_index("occ") * own, own)
    copies[0].wait()
    copies[1].wait()
    dress = jnp.where(unit, 1.0, 0.0) - hole[...]
    total = None
    for j in range(cols):
        padded[j, pl.ds(first, own), :] = given[:, j, :]
        dressed = dot(dress, padded[j])
        chosen = jnp.where((wanted == index) & (inner // kept == j), 1.0, 0.0)
        term = dot(chosen, dressed)
        total = term if j == 0 else total + term
    total = parted(total)
    found = []
    for c in range(2):
        copies[2 + c].wait()
        term = thin_dot(total, parted(lined[c * half : (c + 1) * half, :]), 1)
        found.append(term.reshape(blocks // 2, 2 * cols * kept, half))
    lower = lower_rows(found[0].shape)
    turned = [pltpu.roll(term, cols * kept, 1) for term in found]
    share_ref[:, 0] = jnp.where(lower, found[0], turned[1])
    share_ref[:, 1] = jnp.where(lower, turned[0], found[1])


def share_of(given, lined, hole, blocks):
    naux = lined.shape[0]
    rows = 2 * given.shape[1] * hole.shape[0] // blocks
    return pl.pallas_call(
        share_kernel,
        out_shape=jax.ShapeDtypeStruct((blocks // 2, 2, rows, naux // 2), jnp.float32),
        in_specs=[pl.BlockSpec(memory_space=pl.ANY)] * 3,
        out_specs=pl.BlockSpec(memory_space=pltpu.VMEM),
        scratch_shapes=[
            pltpu.VMEM(given.shape, jnp.float32),
            pltpu.VMEM(lined.shape, jnp.float32),
            pltpu.VMEM(hole.shape, jnp.float32),
            pltpu.VMEM((given.shape[1], hole.shape[0], given.shape[2]), jnp.float32),
            pltpu.SemaphoreType.DMA((4,)),
        ],
    )(given, lined, hole)


def contract_kernel(fitted_ref, factors_ref, ladder_ref):
    halves, rows, half = fitted_ref.shape
    found = fitted_ref[...].reshape(halves // 2, 2, rows, half)
    even, odd = found[:, 0], found[:, 1]
    lower = lower_rows(even.shape)
    parts = (
        jnp.where(lower, even, pltpu.roll(odd, rows // 2, 1)),
        jnp.where(lower, pltpu.roll(even, rows // 2, 1), odd),
    )
    total = None
    for c in range(2):
        fitted = parted(parts[c].reshape(halves * rows // 2, half))
        term = thin_dot(fitted, parted(factors_ref[c * half : (c + 1) * half, :]), 0)
        total = term if c == 0 else total + term
    blocks, rows, _ = ladder_ref.shape
    turned = total.T.reshape(blocks, 2, rows, total.shape[0])
    ladder_ref[...] = jnp.concatenate([turned[:, 0], turned[:, 1]], axis=-1)


def contract(fitted, factors, blocks):
    cols, pairs = fitted.shape[0] * fitted.shape[1] // 2, factors.shape[1]
    return pl.pallas_call(
        contract_kernel,
        out_shape=jax.ShapeDtypeStruct((blocks, pairs // blocks // 2, 2 * cols), jnp.float32),
        in_specs=[pl.BlockSpec(memory_space=pltpu.VMEM)] * 2,
        out_specs=pl.BlockSpec(memory_space=pltpu.VMEM),
        compiler_params=pltpu.CompilerParams(vmem_limit_bytes=room),
    )(fitted, factors)


def finish_kernel(ladder_ref, blocks_ref, out_ref, held):
    lots = blocks_ref.shape[0]
    total = None
    for z in range(lots):
        term = dot(ladder_ref[z], blocks_ref[z])
        total = term if z == 0 else total + term
    halves, kept, norbs = 2, held.shape[0] // 2, out_ref.shape[2]
    rows, cons = out_ref.shape[0] // halves, out_ref.shape[1] // kept
    for s in range(halves * kept):
        held[s] = total[:, s * lanes : (s + 1) * lanes]
    for h in range(halves):
        for i in range(kept):
            for r in range(rows):
                line = held[h * kept + i, pl.ds(r, cons, stride=rows), :]
                out_ref[h * rows + r, pl.ds(i, cons, stride=kept), :] = line[:, :norbs]


def finish(ladder, blocks, shape, kept):
    return pl.pallas_call(
        finish_kernel,
        out_shape=jax.ShapeDtypeStruct(shape, jnp.float32),
        in_specs=[pl.BlockSpec(memory_space=pltpu.VMEM)] * 2,
        out_specs=pl.BlockSpec(memory_space=pltpu.VMEM),
        scratch_shapes=[pltpu.VMEM((2 * kept, ladder.shape[1], lanes), jnp.float32)],
        compiler_params=pltpu.CompilerParams(vmem_limit_bytes=room),
    )(ladder, blocks)


def local(amplitudes, fit_out, fit_con, hole_hole):
    norbs = hole_hole.shape[0]
    naux = fit_con.shape[0]
    halves, lots = lax.axis_size("out_hi"), lax.axis_size("out_lo")
    cons, occs = lax.axis_size("con"), lax.axis_size("occ")
    cols = amplitudes.shape[2]
    kept = norbs // (cons * occs)
    side = lax.axis_index("out_lo")
    dress = jnp.eye(norbs, dtype=jnp.float32) - hole_hole

    share = share_of(jnp.transpose(amplitudes, (1, 2, 0)), fit_con, hole_hole, cons * occs)
    share = share.reshape(cons * occs, *share.shape[2:])
    parts = lax.all_to_all(share, plane, 0, 0, tiled=True)
    fitted = jnp.sum(parts, axis=0)
    whole = lax.all_gather(fitted, "out_hi", axis=0)
    other = lax.ppermute(fit_out, "out_lo", [(0, 1), (1, 0)])
    factors = jnp.concatenate(
        [jnp.where(side == 0, fit_out, other), jnp.where(side == 0, other, fit_out)], axis=1
    )
    factors = jnp.broadcast_to(factors[None], (cons, *factors.shape))
    factors = lax.all_to_all(factors, "con", 0, 0, tiled=True)
    factors = factors.reshape(naux, lots * fit_out.shape[1])
    ladder = contract(whole, factors, lots * cons)
    ladder = lax.all_to_all(ladder, pair, 0, 0, tiled=True)
    rows = fit_out.shape[1] // cons
    ladder = ladder.reshape(lots, cons * rows // 2, lanes)
    orders = jnp.swapaxes(dress.T.reshape(halves, lots, cols, norbs), 0, 1)
    orders = jnp.pad(orders, ((0, 0), (0, 0), (0, 0), (0, lanes - norbs)))
    orders = orders.reshape(lots, 1, halves, cols, 1, 1, 1, lanes)
    same = jnp.eye(2, dtype=jnp.float32).reshape(1, 2, 1, 1, 1, 2, 1, 1)
    kind = jnp.eye(kept, dtype=jnp.float32).reshape(1, 1, 1, 1, kept, 1, kept, 1)
    blocks = (orders * same * kind).reshape(lots, lanes, 2 * kept * lanes)
    return finish(ladder, blocks, (rows, cons * kept, norbs), kept)


def solution(mesh):
    lots = 2
    shape = dict(mesh.shape)
    devices = mesh.devices.reshape(shape["out"] // lots, lots, shape["con"], shape["occ"])
    finer = Mesh(devices, ("out_hi", "out_lo", "con", "occ"))
    out = ("out_hi", "out_lo")
    return jax.shard_map(
        local,
        mesh=finer,
        in_specs=(P("con", "occ", out), P("con", out), P(None, "con"), P()),
        out_specs=P((*out, "con"), "occ", None),
        check_vma=False,
    )
```

```python
import jax
import jax.numpy as jnp
from jax import lax
from jax.experimental import pallas as pl
from jax.experimental.pallas import tpu as pltpu
from jax.sharding import Mesh, PartitionSpec as P

highest = lax.Precision.HIGHEST
con = ("row", "core")
near = ("out_mid", "out_lo")
group = ("out_mid", *con, "occ")
back = (*near, "row")
lanes = 128
room = 16 * 1024 * 1024


def dot(a, b):
    return jnp.dot(a, b, precision=highest, preferred_element_type=jnp.float32)


def parted(a):
    high = a.astype(jnp.bfloat16)
    rest = a - high.astype(jnp.float32)
    middle = rest.astype(jnp.bfloat16)
    return high, middle, (rest - middle.astype(jnp.float32)).astype(jnp.bfloat16)


def narrow(a, b, across):
    return lax.dot_general(a, b, (((1,), (across,)), ((), ())), preferred_element_type=jnp.float32)


def thin_dot(a, parts, across):
    high, middle, low = parts
    rows = a[0].shape[0]
    first = narrow(jnp.concatenate(a, axis=0), high, across)
    second = narrow(jnp.concatenate(a[:2], axis=0), middle, across)
    third = narrow(a[0], low, across)
    small = first[2 * rows :] + second[rows:] + third
    return first[:rows] + (first[rows : 2 * rows] + second[:rows] + small)


def lower_rows(shape):
    return lax.broadcasted_iota(jnp.int32, shape, len(shape) - 2) < shape[-2] // 2


def share_kernel(given_ref, lined_ref, hole_ref, share_ref, given, lined, hole, padded, arrived):
    own, cols, _ = given.shape
    norbs = hole.shape[0]
    blocks = 2 * share_ref.shape[1]
    occs = norbs // own
    kept = norbs // blocks
    sides, cons, depth, width = lined.shape
    quarter = cons * depth // 2
    copies = [
        pltpu.make_async_copy(given_ref, given, arrived.at[0]),
        pltpu.make_async_copy(hole_ref, hole, arrived.at[1]),
    ]
    for c in range(sides):
        copies.append(pltpu.make_async_copy(lined_ref.at[:, c], lined.at[c], arrived.at[2 + c]))
    for copy in copies:
        copy.start()
    padded[...] = jnp.zeros_like(padded)
    place = lax.broadcasted_iota(jnp.int32, (blocks * cols * kept, norbs), 0)
    device, inner = place // (cols * kept), place % (cols * kept)
    wanted = (device % occs) * own + (device // occs) * kept + inner % kept
    index = lax.broadcasted_iota(jnp.int32, (blocks * cols * kept, norbs), 1)
    square = (norbs, norbs)
    unit = lax.broadcasted_iota(jnp.int32, square, 0) == lax.broadcasted_iota(jnp.int32, square, 1)
    first = pl.multiple_of(lax.axis_index("occ") * own, own)
    copies[0].wait()
    copies[1].wait()
    dress = jnp.where(unit, 1.0, 0.0) - hole[...]
    total = None
    for j in range(cols):
        padded[j, pl.ds(first, own), :] = given[:, j, :]
        dressed = dot(dress, padded[j])
        chosen = jnp.where((wanted == index) & (inner // kept == j), 1.0, 0.0)
        term = dot(chosen, dressed)
        total = term if j == 0 else total + term
    total = parted(total)
    for c in range(sides):
        copies[2 + c].wait()
        known = lined[c].reshape(2 * quarter, width)
        found = []
        for q in range(2):
            term = thin_dot(total, parted(known[q * quarter : (q + 1) * quarter]), 1)
            found.append(term.reshape(blocks // 2, 2 * cols * kept, quarter))
        lower = lower_rows(found[0].shape)
        turned = [pltpu.roll(term, cols * kept, 1) for term in found]
        share_ref[c, :, 0] = jnp.where(lower, found[0], turned[1])
        share_ref[c, :, 1] = jnp.where(lower, turned[0], found[1])


def share_of(given, lined, hole, blocks):
    sides, quarter = lined.shape[1], lined.shape[0] * lined.shape[2] // 2
    rows = 2 * given.shape[1] * hole.shape[0] // blocks
    return pl.pallas_call(
        share_kernel,
        out_shape=jax.ShapeDtypeStruct((sides, blocks // 2, 2, rows, quarter), jnp.float32),
        in_specs=[pl.BlockSpec(memory_space=pl.ANY)] * 3,
        out_specs=pl.BlockSpec(memory_space=pltpu.VMEM),
        scratch_shapes=[
            pltpu.VMEM(given.shape, jnp.float32),
            pltpu.VMEM((sides, lined.shape[0], *lined.shape[2:]), jnp.float32),
            pltpu.VMEM(hole.shape, jnp.float32),
            pltpu.VMEM((given.shape[1], hole.shape[0], given.shape[2]), jnp.float32),
            pltpu.SemaphoreType.DMA((4,)),
        ],
    )(given, lined, hole)


def contract_kernel(fitted_ref, factors_ref, ladder_ref):
    halves, rows, half = fitted_ref.shape
    found = fitted_ref[...].reshape(halves // 2, 2, rows, half)
    even, odd = found[:, 0], found[:, 1]
    lower = lower_rows(even.shape)
    parts = (
        jnp.where(lower, even, pltpu.roll(odd, rows // 2, 1)),
        jnp.where(lower, pltpu.roll(even, rows // 2, 1), odd),
    )
    total = None
    for c in range(2):
        fitted = parted(parts[c].reshape(halves * rows // 2, half))
        term = thin_dot(fitted, parted(factors_ref[c * half : (c + 1) * half, :]), 0)
        total = term if c == 0 else total + term
    ladder_ref[...] = total.T.reshape(ladder_ref.shape)


def contract(fitted, factors, blocks):
    cols, pairs = fitted.shape[0] * fitted.shape[1] // 2, factors.shape[1]
    return pl.pallas_call(
        contract_kernel,
        out_shape=jax.ShapeDtypeStruct((blocks, pairs // blocks, cols), jnp.float32),
        in_specs=[pl.BlockSpec(memory_space=pltpu.VMEM)] * 2,
        out_specs=pl.BlockSpec(memory_space=pltpu.VMEM),
        compiler_params=pltpu.CompilerParams(vmem_limit_bytes=room),
    )(fitted, factors)


def finish_kernel(ladder_ref, blocks_ref, out_ref, held):
    lots = blocks_ref.shape[0]
    total = None
    for z in range(lots):
        term = thin_dot(parted(ladder_ref[0, z] + ladder_ref[1, z]), parted(blocks_ref[z]), 0)
        total = term if z == 0 else total + term
    kinds = held.shape[0]
    rows, _, norbs = out_ref.shape
    lines = out_ref.shape[1] // kinds
    for s in range(kinds):
        held[s] = total[:, s * lanes : (s + 1) * lanes]
    for s in range(kinds):
        for r in range(rows):
            line = held[s, pl.ds(r, lines, stride=rows), :]
            out_ref[r, pl.ds(s, lines, stride=kinds), :] = line[:, :norbs]


def finish(ladder, blocks, shape):
    kinds = blocks.shape[2] // lanes
    return pl.pallas_call(
        finish_kernel,
        out_shape=jax.ShapeDtypeStruct(shape, jnp.float32),
        in_specs=[pl.BlockSpec(memory_space=pltpu.VMEM)] * 2,
        out_specs=pl.BlockSpec(memory_space=pltpu.VMEM),
        scratch_shapes=[pltpu.VMEM((kinds, ladder.shape[2], lanes), jnp.float32)],
        compiler_params=pltpu.CompilerParams(vmem_limit_bytes=room),
    )(ladder, blocks)


def exchanged(array, flip):
    return lax.ppermute(array, near, [(k, k ^ flip) for k in range(4)])


def local(amplitudes, fit_out, fit_con, hole_hole):
    norbs = hole_hole.shape[0]
    naux = fit_con.shape[0]
    highs, mids, lots = lax.axis_size("out_hi"), lax.axis_size("out_mid"), lax.axis_size("out_lo")
    lines, cores, occs = lax.axis_size("row"), lax.axis_size("core"), lax.axis_size("occ")
    cons = lines * cores
    cols = amplitudes.shape[2]
    kept = norbs // (cons * occs)
    pairs = fit_out.shape[1]
    rows = pairs // cons
    depth = naux // cons // mids
    mid, low = lax.axis_index("out_mid"), lax.axis_index("out_lo")
    dress = jnp.eye(norbs, dtype=jnp.float32) - hole_hole

    lined = fit_con.reshape(cons, mids, depth, fit_con.shape[1])
    share = share_of(jnp.transpose(amplitudes, (1, 2, 0)), lined, hole_hole, cons * occs)
    share = share.reshape(mids * cons * occs, *share.shape[3:])
    parts = lax.all_to_all(share, group, 0, 0, tiled=True)
    parts = parts.reshape(mids, cons * occs, *parts.shape[1:])
    fitted = jnp.sum(parts, axis=1).reshape(-1, parts.shape[3])
    whole = lax.all_gather(fitted, ("out_hi", "core"), axis=0)
    whole = whole.reshape(highs * cores * mids, -1, whole.shape[2])
    index = jnp.arange(pairs)
    origin = (index // rows % lines * cores + index // (rows * lines)) * rows + index % rows
    chosen = (index[:, None] == origin[None]).astype(jnp.float32)
    mine = jnp.dot(fit_out, chosen, precision=highest).reshape(mids, depth, pairs)
    near_half = jnp.where(mid == 0, mine[0], mine[1])
    far_half = jnp.where(mid == 0, mine[1], mine[0])
    found = [near_half, exchanged(near_half, 1), exchanged(far_half, 2), exchanged(far_half, 3)]
    found = [jnp.where(low == 0, found[k], found[k ^ 1]) for k in range(4)]
    found = [jnp.where(mid == 0, found[k], found[k ^ 2]) for k in range(4)]
    wide = pairs // cores
    factors = jnp.stack(
        [jnp.concatenate([p[:, c * wide : (c + 1) * wide] for p in found], axis=1) for c in range(cores)]
    )
    factors = jnp.broadcast_to(factors[None], (lines, *factors.shape))
    factors = lax.all_to_all(factors.reshape(cons, *factors.shape[2:]), con, 0, 0, tiled=True)
    factors = factors.reshape(cons * depth, mids * lots * wide)
    ladder = contract(whole, factors, mids * lots * lines)
    ladder = lax.all_to_all(ladder, back, 0, 0, tiled=True)
    ladder = ladder.reshape(mids, lots, lines * rows, lanes)
    orders = jnp.transpose(dress.T.reshape(highs, mids, lots, cols, norbs), (2, 0, 1, 3, 4))
    orders = jnp.pad(orders, ((0, 0),) * 4 + ((0, lanes - norbs),))
    orders = orders.reshape(lots, highs, 1, mids, cols, 1, 1, 1, lanes)
    same = jnp.eye(cores, dtype=jnp.float32).reshape(1, 1, cores, 1, 1, 1, cores, 1, 1)
    kind = jnp.eye(kept, dtype=jnp.float32).reshape(1, 1, 1, 1, 1, kept, 1, kept, 1)
    blocks = (orders * same * kind).reshape(lots, lanes, cores * kept * lanes)
    return finish(ladder, blocks, (rows, cons * kept, norbs))


def solution(mesh):
    shape = dict(mesh.shape)
    sizes = (shape["out"] // 4, 2, 2, shape["con"] // 2, 2, shape["occ"])
    finer = Mesh(mesh.devices.reshape(sizes), ("out_hi", *near, *con, "occ"))
    out = ("out_hi", *near)
    return jax.shard_map(
        local,
        mesh=finer,
        in_specs=(P(con, "occ", out), P(con, out), P(None, con), P()),
        out_specs=P((*out, *con), "occ", None),
        check_vma=False,
    )
```

```python
import jax
import jax.numpy as jnp
from jax import lax
from jax.experimental import pallas as pl
from jax.experimental.pallas import tpu as pltpu
from jax.sharding import Mesh, PartitionSpec as P

highest = lax.Precision.HIGHEST
con = ("row", "core")
plane = ("row", "core", "occ")
pair = ("out_lo", "row")
lanes = 128
room = 16 * 1024 * 1024


def dot(a, b):
    return jnp.dot(a, b, precision=highest, preferred_element_type=jnp.float32)


def parted(a):
    high = a.astype(jnp.bfloat16)
    rest = a - high.astype(jnp.float32)
    middle = rest.astype(jnp.bfloat16)
    return high, middle, (rest - middle.astype(jnp.float32)).astype(jnp.bfloat16)


def narrow(a, b, across):
    return lax.dot_general(a, b, (((1,), (across,)), ((), ())), preferred_element_type=jnp.float32)


def thin_dot(a, parts, across):
    high, middle, low = parts
    rows = a[0].shape[0]
    first = narrow(jnp.concatenate(a, axis=0), high, across)
    second = narrow(jnp.concatenate(a[:2], axis=0), middle, across)
    third = narrow(a[0], low, across)
    small = first[2 * rows :] + second[rows:] + third
    return first[:rows] + (first[rows : 2 * rows] + second[:rows] + small)


def lower_rows(shape):
    return lax.broadcasted_iota(jnp.int32, shape, len(shape) - 2) < shape[-2] // 2


def share_kernel(given_ref, lined_ref, hole_ref, share_ref, given, lined, hole, padded, arrived):
    own, cols, _ = given.shape
    norbs = hole.shape[0]
    blocks = 2 * share_ref.shape[0]
    occs = norbs // own
    kept = norbs // blocks
    half = lined.shape[0] // 2
    copies = [
        pltpu.make_async_copy(given_ref, given, arrived.at[0]),
        pltpu.make_async_copy(hole_ref, hole, arrived.at[1]),
    ]
    for c in range(2):
        rows = pl.ds(c * half, half)
        copies.append(pltpu.make_async_copy(lined_ref.at[rows, :], lined.at[rows, :], arrived.at[2 + c]))
    for copy in copies:
        copy.start()
    padded[...] = jnp.zeros_like(padded)
    place = lax.broadcasted_iota(jnp.int32, (blocks * cols * kept, norbs), 0)
    device, inner = place // (cols * kept), place % (cols * kept)
    wanted = (device % occs) * own + (device // occs) * kept + inner % kept
    index = lax.broadcasted_iota(jnp.int32, (blocks * cols * kept, norbs), 1)
    square = (norbs, norbs)
    unit = lax.broadcasted_iota(jnp.int32, square, 0) == lax.broadcasted_iota(jnp.int32, square, 1)
    first = pl.multiple_of(lax.axis_index("occ") * own, own)
    copies[0].wait()
    copies[1].wait()
    dress = jnp.where(unit, 1.0, 0.0) - hole[...]
    total = None
    for j in range(cols):
        padded[j, pl.ds(first, own), :] = given[:, j, :]
        dressed = dot(dress, padded[j])
        chosen = jnp.where((wanted == index) & (inner // kept == j), 1.0, 0.0)
        term = dot(chosen, dressed)
        total = term if j == 0 else total + term
    total = parted(total)
    found = []
    for c in range(2):
        copies[2 + c].wait()
        term = thin_dot(total, parted(lined[c * half : (c + 1) * half, :]), 1)
        found.append(term.reshape(blocks // 2, 2 * cols * kept, half))
    lower = lower_rows(found[0].shape)
    turned = [pltpu.roll(term, cols * kept, 1) for term in found]
    share_ref[:, 0] = jnp.where(lower, found[0], turned[1])
    share_ref[:, 1] = jnp.where(lower, turned[0], found[1])


def share_of(given, lined, hole, blocks):
    naux = lined.shape[0]
    rows = 2 * given.shape[1] * hole.shape[0] // blocks
    return pl.pallas_call(
        share_kernel,
        out_shape=jax.ShapeDtypeStruct((blocks // 2, 2, rows, naux // 2), jnp.float32),
        in_specs=[pl.BlockSpec(memory_space=pl.ANY)] * 3,
        out_specs=pl.BlockSpec(memory_space=pltpu.VMEM),
        scratch_shapes=[
            pltpu.VMEM(given.shape, jnp.float32),
            pltpu.VMEM(lined.shape, jnp.float32),
            pltpu.VMEM(hole.shape, jnp.float32),
            pltpu.VMEM((given.shape[1], hole.shape[0], given.shape[2]), jnp.float32),
            pltpu.SemaphoreType.DMA((4,)),
        ],
    )(given, lined, hole)


def contract_kernel(fitted_ref, factors_ref, ladder_ref):
    halves, rows, half = fitted_ref.shape
    found = fitted_ref[...].reshape(halves // 2, 2, rows, half)
    even, odd = found[:, 0], found[:, 1]
    lower = lower_rows(even.shape)
    parts = (
        jnp.where(lower, even, pltpu.roll(odd, rows // 2, 1)),
        jnp.where(lower, pltpu.roll(even, rows // 2, 1), odd),
    )
    total = None
    for c in range(2):
        fitted = parted(parts[c].reshape(halves * rows // 2, half))
        term = thin_dot(fitted, parted(factors_ref[c * half : (c + 1) * half, :]), 0)
        total = term if c == 0 else total + term
    ladder_ref[...] = total.T.reshape(ladder_ref.shape)


def contract(fitted, factors, blocks):
    cols, pairs = fitted.shape[0] * fitted.shape[1] // 2, factors.shape[1]
    return pl.pallas_call(
        contract_kernel,
        out_shape=jax.ShapeDtypeStruct((blocks, pairs // blocks, cols), jnp.float32),
        in_specs=[pl.BlockSpec(memory_space=pltpu.VMEM)] * 2,
        out_specs=pl.BlockSpec(memory_space=pltpu.VMEM),
        compiler_params=pltpu.CompilerParams(vmem_limit_bytes=room),
    )(fitted, factors)


def finish_kernel(ladder_ref, blocks_ref, out_ref, held):
    lots = blocks_ref.shape[0]
    total = None
    for z in range(lots):
        term = thin_dot(parted(ladder_ref[z]), parted(blocks_ref[z]), 0)
        total = term if z == 0 else total + term
    kinds = held.shape[0]
    rows, _, norbs = out_ref.shape
    lines = out_ref.shape[1] // kinds
    for s in range(kinds):
        held[s] = total[:, s * lanes : (s + 1) * lanes]
    for s in range(kinds):
        for r in range(rows):
            line = held[s, pl.ds(r, lines, stride=rows), :]
            out_ref[r, pl.ds(s, lines, stride=kinds), :] = line[:, :norbs]


def finish(ladder, blocks, shape):
    kinds = blocks.shape[2] // lanes
    return pl.pallas_call(
        finish_kernel,
        out_shape=jax.ShapeDtypeStruct(shape, jnp.float32),
        in_specs=[pl.BlockSpec(memory_space=pltpu.VMEM)] * 2,
        out_specs=pl.BlockSpec(memory_space=pltpu.VMEM),
        scratch_shapes=[pltpu.VMEM((kinds, ladder.shape[1], lanes), jnp.float32)],
        compiler_params=pltpu.CompilerParams(vmem_limit_bytes=room),
    )(ladder, blocks)


def local(amplitudes, fit_out, fit_con, hole_hole):
    norbs = hole_hole.shape[0]
    naux = fit_con.shape[0]
    halves, lots = lax.axis_size("out_hi"), lax.axis_size("out_lo")
    lines, cores, occs = lax.axis_size("row"), lax.axis_size("core"), lax.axis_size("occ")
    cons = lines * cores
    cols = amplitudes.shape[2]
    kept = norbs // (cons * occs)
    _, pairs = fit_out.shape
    rows = pairs // cons
    side = lax.axis_index("out_lo")
    dress = jnp.eye(norbs, dtype=jnp.float32) - hole_hole

    share = share_of(jnp.transpose(amplitudes, (1, 2, 0)), fit_con, hole_hole, cons * occs)
    share = share.reshape(cons * occs, *share.shape[2:])
    parts = lax.all_to_all(share, plane, 0, 0, tiled=True)
    fitted = jnp.sum(parts, axis=0)
    whole = lax.all_gather(fitted, ("out_hi", "core"), axis=0)
    index = jnp.arange(pairs)
    origin = (index // rows % lines * cores + index // (rows * lines)) * rows + index % rows
    chosen = (index[:, None] == origin[None]).astype(jnp.float32)
    mine = jnp.dot(fit_out, chosen, precision=highest)
    other = lax.ppermute(mine, "out_lo", [(0, 1), (1, 0)])
    planes = [jnp.where(side == 0, mine, other), jnp.where(side == 0, other, mine)]
    wide = pairs // cores
    factors = jnp.stack(
        [jnp.concatenate([p[:, c * wide : (c + 1) * wide] for p in planes], axis=1) for c in range(cores)]
    )
    factors = jnp.broadcast_to(factors[None], (lines, *factors.shape))
    factors = lax.all_to_all(factors.reshape(cons, *factors.shape[2:]), con, 0, 0, tiled=True)
    factors = factors.reshape(naux, lots * wide)
    ladder = contract(whole, factors, lots * lines)
    ladder = lax.all_to_all(ladder, pair, 0, 0, tiled=True)
    ladder = ladder.reshape(lots, lines * rows, lanes)
    orders = jnp.swapaxes(dress.T.reshape(halves, lots, cols, norbs), 0, 1)
    orders = jnp.pad(orders, ((0, 0), (0, 0), (0, 0), (0, lanes - norbs)))
    orders = orders.reshape(lots, halves, 1, cols, 1, 1, 1, lanes)
    same = jnp.eye(cores, dtype=jnp.float32).reshape(1, 1, cores, 1, 1, cores, 1, 1)
    kind = jnp.eye(kept, dtype=jnp.float32).reshape(1, 1, 1, 1, kept, 1, kept, 1)
    blocks = (orders * same * kind).reshape(lots, lanes, cores * kept * lanes)
    return finish(ladder, blocks, (rows, cons * kept, norbs))


def solution(mesh):
    lots, cores = 2, 2
    shape = dict(mesh.shape)
    devices = mesh.devices.reshape(shape["out"] // lots, lots, shape["con"] // cores, cores, shape["occ"])
    finer = Mesh(devices, ("out_hi", "out_lo", *con, "occ"))
    out = ("out_hi", "out_lo")
    return jax.shard_map(
        local,
        mesh=finer,
        in_specs=(P(con, "occ", out), P(con, out), P(None, con), P()),
        out_specs=P((*out, *con), "occ", None),
        check_vma=False,
    )
```

```python
import jax
import jax.numpy as jnp
from jax import lax
from jax.experimental import pallas as pl
from jax.experimental.pallas import tpu as pltpu
from jax.sharding import Mesh, PartitionSpec as P

highest = lax.Precision.HIGHEST
con = ("row", "core")
plane = ("row", "core", "occ")
pair = ("out_lo", "row")
lanes = 128
room = 16 * 1024 * 1024


def dot(a, b):
    return jnp.dot(a, b, precision=highest, preferred_element_type=jnp.float32)


def parted(a):
    high = a.astype(jnp.bfloat16)
    rest = a - high.astype(jnp.float32)
    middle = rest.astype(jnp.bfloat16)
    return high, middle, (rest - middle.astype(jnp.float32)).astype(jnp.bfloat16)


def narrow(a, b, across):
    return lax.dot_general(a, b, (((1,), (across,)), ((), ())), preferred_element_type=jnp.float32)


def thin_dot(a, parts, across):
    high, middle, low = parts
    rows = a[0].shape[0]
    first = narrow(jnp.concatenate(a, axis=0), high, across)
    second = narrow(jnp.concatenate(a[:2], axis=0), middle, across)
    third = narrow(a[0], low, across)
    small = first[2 * rows :] + second[rows:] + third
    return first[:rows] + (first[rows : 2 * rows] + second[:rows] + small)


def lower_rows(shape):
    return lax.broadcasted_iota(jnp.int32, shape, len(shape) - 2) < shape[-2] // 2


def share_kernel(given_ref, lined_ref, hole_ref, share_ref, given, lined, hole, padded, share, arrived, left):
    own, cols, width = given.shape
    norbs = hole.shape[0]
    steps, _, chunk, _ = lined.shape
    blocks = 2 * share.shape[0]
    occs = norbs // own
    kept = norbs // blocks
    copies = [
        pltpu.make_async_copy(given_ref, given, arrived.at[0]),
        pltpu.make_async_copy(hole_ref, hole, arrived.at[1]),
    ]
    for q in range(steps):
        copies.append(pltpu.make_async_copy(lined_ref.at[:, q], lined.at[q], arrived.at[2 + q]))
    for copy in copies:
        copy.start()
    padded[...] = jnp.zeros_like(padded)
    square = (blocks * cols * kept, cols * norbs)
    place = lax.broadcasted_iota(jnp.int32, square, 0)
    index = lax.broadcasted_iota(jnp.int32, square, 1)
    device, inner = place // (cols * kept), place % (cols * kept)
    wanted = (device % occs) * own + (device // occs) * kept + inner % kept + inner // kept * norbs
    chosen = jnp.where(wanted == index, 1.0, 0.0).astype(jnp.bfloat16)
    square = (norbs, norbs)
    unit = lax.broadcasted_iota(jnp.int32, square, 0) == lax.broadcasted_iota(jnp.int32, square, 1)
    first = pl.multiple_of(lax.axis_index("occ") * own, own)
    copies[0].wait()
    for j in range(cols):
        padded[pl.ds(first, own), j * width : (j + 1) * width] = given[:, j, :]
    copies[1].wait()
    dressed = dot(jnp.where(unit, 1.0, 0.0) - hole[...], padded[...])
    dressed = jnp.concatenate([dressed[:, j * width : (j + 1) * width] for j in range(cols)], axis=0)
    picked = narrow(chosen, jnp.concatenate(parted(dressed), axis=1), 0)
    total = tuple(picked[:, k * width : (k + 1) * width].astype(jnp.bfloat16) for k in range(3))
    sends = []
    for q in range(steps):
        copies[2 + q].wait()
        term = thin_dot(total, parted(lined[q].reshape(2 * chunk, width)), 1)
        found = [
            term[:, c * chunk : (c + 1) * chunk].reshape(blocks // 2, 2 * cols * kept, chunk) for c in range(2)
        ]
        lower = lower_rows(found[0].shape)
        turned = [pltpu.roll(part, cols * kept, 1) for part in found]
        lot = pl.ds(q * chunk, chunk)
        share[:, 0, :, q * chunk : (q + 1) * chunk] = jnp.where(lower, found[0], turned[1])
        share[:, 1, :, q * chunk : (q + 1) * chunk] = jnp.where(lower, turned[0], found[1])
        sends.append(
            pltpu.make_async_copy(share.at[:, :, :, lot], share_ref.at[:, :, :, lot], left.at[q])
        )
        sends[-1].start()
    for send in sends:
        send.wait()


def share_of(given, lined, hole, blocks):
    steps = 4
    naux, width = lined.shape
    rows = 2 * given.shape[1] * hole.shape[0] // blocks
    shape = (blocks // 2, 2, rows, naux // 2)
    chunk = naux // 2 // steps
    return pl.pallas_call(
        share_kernel,
        out_shape=jax.ShapeDtypeStruct(shape, jnp.float32),
        in_specs=[pl.BlockSpec(memory_space=pl.ANY)] * 3,
        out_specs=pl.BlockSpec(memory_space=pl.ANY),
        scratch_shapes=[
            pltpu.VMEM(given.shape, jnp.float32),
            pltpu.VMEM((steps, 2, chunk, width), jnp.float32),
            pltpu.VMEM(hole.shape, jnp.float32),
            pltpu.VMEM((hole.shape[0], given.shape[1] * given.shape[2]), jnp.float32),
            pltpu.VMEM(shape, jnp.float32),
            pltpu.SemaphoreType.DMA((2 + steps,)),
            pltpu.SemaphoreType.DMA((steps,)),
        ],
    )(given, lined.reshape(2, steps, chunk, width), hole)


def contract_kernel(fitted_ref, factors_ref, ladder_ref):
    halves, rows, half = fitted_ref.shape
    found = fitted_ref[...].reshape(halves // 2, 2, rows, half)
    even, odd = found[:, 0], found[:, 1]
    lower = lower_rows(even.shape)
    parts = (
        jnp.where(lower, even, pltpu.roll(odd, rows // 2, 1)),
        jnp.where(lower, pltpu.roll(even, rows // 2, 1), odd),
    )
    total = None
    for c in range(2):
        fitted = parted(parts[c].reshape(halves * rows // 2, half))
        term = thin_dot(fitted, parted(factors_ref[c * half : (c + 1) * half, :]), 0)
        total = term if c == 0 else total + term
    ladder_ref[...] = total.T.reshape(ladder_ref.shape)


def contract(fitted, factors, blocks):
    cols, pairs = fitted.shape[0] * fitted.shape[1] // 2, factors.shape[1]
    return pl.pallas_call(
        contract_kernel,
        out_shape=jax.ShapeDtypeStruct((blocks, pairs // blocks, cols), jnp.float32),
        in_specs=[pl.BlockSpec(memory_space=pltpu.VMEM)] * 2,
        out_specs=pl.BlockSpec(memory_space=pltpu.VMEM),
        compiler_params=pltpu.CompilerParams(vmem_limit_bytes=room),
    )(fitted, factors)


def pieces_kernel(blocks_ref, pieces_ref):
    for k, piece in enumerate(parted(blocks_ref[...])):
        pieces_ref[k] = piece


def pieces_of(blocks):
    return pl.pallas_call(
        pieces_kernel,
        out_shape=jax.ShapeDtypeStruct((3, *blocks.shape), jnp.bfloat16),
        in_specs=[pl.BlockSpec(memory_space=pltpu.VMEM)],
        out_specs=pl.BlockSpec(memory_space=pltpu.VMEM),
        compiler_params=pltpu.CompilerParams(vmem_limit_bytes=room),
    )(blocks)


def finish_kernel(ladder_ref, blocks_ref, out_ref, held):
    lots = blocks_ref.shape[1]
    total = None
    for z in range(lots):
        term = thin_dot(parted(ladder_ref[z]), tuple(blocks_ref[k, z] for k in range(3)), 0)
        total = term if z == 0 else total + term
    kinds = held.shape[0]
    rows, _, norbs = out_ref.shape
    lines = out_ref.shape[1] // kinds
    for s in range(kinds):
        held[s] = total[:, s * lanes : (s + 1) * lanes]
    for s in range(kinds):
        for r in range(rows):
            line = held[s, pl.ds(r, lines, stride=rows), :]
            out_ref[r, pl.ds(s, lines, stride=kinds), :] = line[:, :norbs]


def finish(ladder, blocks, shape):
    kinds = blocks.shape[3] // lanes
    return pl.pallas_call(
        finish_kernel,
        out_shape=jax.ShapeDtypeStruct(shape, jnp.float32),
        in_specs=[pl.BlockSpec(memory_space=pltpu.VMEM)] * 2,
        out_specs=pl.BlockSpec(memory_space=pltpu.VMEM),
        scratch_shapes=[pltpu.VMEM((kinds, ladder.shape[1], lanes), jnp.float32)],
        compiler_params=pltpu.CompilerParams(vmem_limit_bytes=room),
    )(ladder, blocks)


def local(amplitudes, fit_out, fit_con, hole_hole):
    norbs = hole_hole.shape[0]
    naux = fit_con.shape[0]
    halves, lots = lax.axis_size("out_hi"), lax.axis_size("out_lo")
    lines, cores, occs = lax.axis_size("row"), lax.axis_size("core"), lax.axis_size("occ")
    cons = lines * cores
    cols = amplitudes.shape[2]
    kept = norbs // (cons * occs)
    _, pairs = fit_out.shape
    rows = pairs // cons
    side = lax.axis_index("out_lo")
    dress = jnp.eye(norbs, dtype=jnp.float32) - hole_hole

    share = share_of(jnp.transpose(amplitudes, (1, 2, 0)), fit_con, hole_hole, cons * occs)
    share = share.reshape(cons * occs, *share.shape[2:])
    parts = lax.all_to_all(share, plane, 0, 0, tiled=True)
    fitted = jnp.sum(parts, axis=0)
    whole = lax.all_gather(fitted, ("out_hi", "core"), axis=0)
    index = jnp.arange(pairs)
    origin = (index // rows % lines * cores + index // (rows * lines)) * rows + index % rows
    chosen = (index[:, None] == origin[None]).astype(jnp.float32)
    mine = jnp.dot(fit_out, chosen, precision=highest)
    other = lax.ppermute(mine, "out_lo", [(0, 1), (1, 0)])
    planes = [jnp.where(side == 0, mine, other), jnp.where(side == 0, other, mine)]
    wide = pairs // cores
    factors = jnp.stack(
        [jnp.concatenate([p[:, c * wide : (c + 1) * wide] for p in planes], axis=1) for c in range(cores)]
    )
    factors = jnp.broadcast_to(factors[None], (lines, *factors.shape))
    factors = lax.all_to_all(factors.reshape(cons, *factors.shape[2:]), con, 0, 0, tiled=True)
    factors = factors.reshape(naux, lots * wide)
    ladder = contract(whole, factors, lots * lines)
    ladder = lax.all_to_all(ladder, pair, 0, 0, tiled=True)
    ladder = ladder.reshape(lots, lines * rows, lanes)
    orders = jnp.swapaxes(dress.T.reshape(halves, lots, cols, norbs), 0, 1)
    orders = jnp.pad(orders, ((0, 0), (0, 0), (0, 0), (0, lanes - norbs)))
    orders = orders.reshape(lots, halves, 1, cols, 1, 1, 1, lanes)
    same = jnp.eye(cores, dtype=jnp.float32).reshape(1, 1, cores, 1, 1, cores, 1, 1)
    kind = jnp.eye(kept, dtype=jnp.float32).reshape(1, 1, 1, 1, kept, 1, kept, 1)
    blocks = (orders * same * kind).reshape(lots, lanes, cores * kept * lanes)
    blocks = pieces_of(blocks)
    return finish(ladder, blocks, (rows, cons * kept, norbs))


def solution(mesh):
    lots, cores = 2, 2
    shape = dict(mesh.shape)
    devices = mesh.devices.reshape(shape["out"] // lots, lots, shape["con"] // cores, cores, shape["occ"])
    finer = Mesh(devices, ("out_hi", "out_lo", *con, "occ"))
    out = ("out_hi", "out_lo")
    return jax.shard_map(
        local,
        mesh=finer,
        in_specs=(P(con, "occ", out), P(con, out), P(None, con), P()),
        out_specs=P((*out, *con), "occ", None),
        check_vma=False,
    )
```

```python
import jax
import jax.numpy as jnp
from jax import lax
from jax.experimental import pallas as pl
from jax.experimental.pallas import tpu as pltpu
from jax.sharding import Mesh, PartitionSpec as P

highest = lax.Precision.HIGHEST
con = ("row", "core")
plane = ("row", "core", "occ")
pair = ("out_lo", "row")
lanes = 128
room = 16 * 1024 * 1024


def dot(a, b):
    return jnp.dot(a, b, precision=highest, preferred_element_type=jnp.float32)


def parted(a):
    high = a.astype(jnp.bfloat16)
    rest = a - high.astype(jnp.float32)
    middle = rest.astype(jnp.bfloat16)
    return high, middle, (rest - middle.astype(jnp.float32)).astype(jnp.bfloat16)


def narrow(a, b, across):
    return lax.dot_general(a, b, (((1,), (across,)), ((), ())), preferred_element_type=jnp.float32)


def thin_dot(a, parts, across):
    high, middle, low = parts
    rows = a[0].shape[0]
    first = narrow(jnp.concatenate(a, axis=0), high, across)
    second = narrow(jnp.concatenate(a[:2], axis=0), middle, across)
    third = narrow(a[0], low, across)
    small = first[2 * rows :] + second[rows:] + third
    return first[:rows] + (first[rows : 2 * rows] + second[:rows] + small)


def lower_rows(shape):
    return lax.broadcasted_iota(jnp.int32, shape, len(shape) - 2) < shape[-2] // 2


def share_kernel(given_ref, lined_ref, hole_ref, share_ref, given, lined, hole, padded, share, arrived, left):
    own, cols, width = given.shape
    norbs = hole.shape[0]
    steps, _, chunk, _ = lined.shape
    blocks = 2 * share.shape[0]
    occs = norbs // own
    kept = norbs // blocks
    copies = [
        pltpu.make_async_copy(given_ref, given, arrived.at[0]),
        pltpu.make_async_copy(hole_ref, hole, arrived.at[1]),
    ]
    for q in range(steps):
        copies.append(pltpu.make_async_copy(lined_ref.at[:, q], lined.at[q], arrived.at[2 + q]))
    for copy in copies:
        copy.start()
    padded[...] = jnp.zeros_like(padded)
    square = (blocks * cols * kept, cols * norbs)
    place = lax.broadcasted_iota(jnp.int32, square, 0)
    index = lax.broadcasted_iota(jnp.int32, square, 1)
    device, inner = place // (cols * kept), place % (cols * kept)
    wanted = (device % occs) * own + (device // occs) * kept + inner % kept + inner // kept * norbs
    chosen = jnp.where(wanted == index, 1.0, 0.0).astype(jnp.bfloat16)
    square = (norbs, norbs)
    unit = lax.broadcasted_iota(jnp.int32, square, 0) == lax.broadcasted_iota(jnp.int32, square, 1)
    first = pl.multiple_of(lax.axis_index("occ") * own, own)
    copies[0].wait()
    for j in range(cols):
        padded[pl.ds(first, own), j * width : (j + 1) * width] = given[:, j, :]
    copies[1].wait()
    dressed = dot(jnp.where(unit, 1.0, 0.0) - hole[...], padded[...])
    dressed = jnp.concatenate([dressed[:, j * width : (j + 1) * width] for j in range(cols)], axis=0)
    picked = narrow(chosen, jnp.concatenate(parted(dressed), axis=1), 0)
    total = tuple(picked[:, k * width : (k + 1) * width].astype(jnp.bfloat16) for k in range(3))
    sends = []
    for q in range(steps):
        copies[2 + q].wait()
        term = thin_dot(total, parted(lined[q].reshape(2 * chunk, width)), 1)
        found = [
            term[:, c * chunk : (c + 1) * chunk].reshape(blocks // 2, 2 * cols * kept, chunk) for c in range(2)
        ]
        lower = lower_rows(found[0].shape)
        turned = [pltpu.roll(part, cols * kept, 1) for part in found]
        lot = pl.ds(q * chunk, chunk)
        share[:, 0, :, q * chunk : (q + 1) * chunk] = jnp.where(lower, found[0], turned[1])
        share[:, 1, :, q * chunk : (q + 1) * chunk] = jnp.where(lower, turned[0], found[1])
        sends.append(
            pltpu.make_async_copy(share.at[:, :, :, lot], share_ref.at[:, :, :, lot], left.at[q])
        )
        sends[-1].start()
    for send in sends:
        send.wait()


def share_of(given, lined, hole, blocks):
    steps = 4
    naux, width = lined.shape
    rows = 2 * given.shape[1] * hole.shape[0] // blocks
    shape = (blocks // 2, 2, rows, naux // 2)
    chunk = naux // 2 // steps
    return pl.pallas_call(
        share_kernel,
        out_shape=jax.ShapeDtypeStruct(shape, jnp.float32),
        in_specs=[pl.BlockSpec(memory_space=pl.ANY)] * 3,
        out_specs=pl.BlockSpec(memory_space=pl.ANY),
        scratch_shapes=[
            pltpu.VMEM(given.shape, jnp.float32),
            pltpu.VMEM((steps, 2, chunk, width), jnp.float32),
            pltpu.VMEM(hole.shape, jnp.float32),
            pltpu.VMEM((hole.shape[0], given.shape[1] * given.shape[2]), jnp.float32),
            pltpu.VMEM(shape, jnp.float32),
            pltpu.SemaphoreType.DMA((2 + steps,)),
            pltpu.SemaphoreType.DMA((steps,)),
        ],
    )(given, lined.reshape(2, steps, chunk, width), hole)


def contract_kernel(fitted_ref, factors_ref, ladder_ref):
    halves, rows, half = fitted_ref.shape
    found = fitted_ref[...].reshape(halves // 2, 2, rows, half)
    even, odd = found[:, 0], found[:, 1]
    lower = lower_rows(even.shape)
    parts = (
        jnp.where(lower, even, pltpu.roll(odd, rows // 2, 1)),
        jnp.where(lower, pltpu.roll(even, rows // 2, 1), odd),
    )
    total = None
    for c in range(2):
        fitted = parted(parts[c].reshape(halves * rows // 2, half))
        term = thin_dot(fitted, parted(factors_ref[c * half : (c + 1) * half, :]), 0)
        total = term if c == 0 else total + term
    ladder_ref[...] = total.T.reshape(ladder_ref.shape)


def contract(fitted, factors, blocks):
    cols, pairs = fitted.shape[0] * fitted.shape[1] // 2, factors.shape[1]
    return pl.pallas_call(
        contract_kernel,
        out_shape=jax.ShapeDtypeStruct((blocks, pairs // blocks, cols), jnp.float32),
        in_specs=[pl.BlockSpec(memory_space=pltpu.VMEM)] * 2,
        out_specs=pl.BlockSpec(memory_space=pltpu.VMEM),
        compiler_params=pltpu.CompilerParams(vmem_limit_bytes=room),
    )(fitted, factors)


def pieces_kernel(blocks_ref, pieces_ref):
    for k, piece in enumerate(parted(blocks_ref[...])):
        pieces_ref[k] = piece


def pieces_of(blocks):
    return pl.pallas_call(
        pieces_kernel,
        out_shape=jax.ShapeDtypeStruct((3, *blocks.shape), jnp.bfloat16),
        in_specs=[pl.BlockSpec(memory_space=pltpu.VMEM)],
        out_specs=pl.BlockSpec(memory_space=pltpu.VMEM),
        compiler_params=pltpu.CompilerParams(vmem_limit_bytes=room),
    )(blocks)


def finish_kernel(ladder_ref, blocks_ref, out_ref, held):
    lots = blocks_ref.shape[1]
    total = None
    for z in range(lots):
        term = thin_dot(parted(ladder_ref[z]), tuple(blocks_ref[k, z] for k in range(3)), 0)
        total = term if z == 0 else total + term
    kinds = held.shape[0]
    rows, _, norbs = out_ref.shape
    lines = out_ref.shape[1] // kinds
    for s in range(kinds):
        held[s] = total[:, s * lanes : (s + 1) * lanes]
    for s in range(kinds):
        for r in range(rows):
            line = held[s, pl.ds(r, lines, stride=rows), :]
            out_ref[r, pl.ds(s, lines, stride=kinds), :] = line[:, :norbs]


def finish(ladder, blocks, shape):
    kinds = blocks.shape[3] // lanes
    return pl.pallas_call(
        finish_kernel,
        out_shape=jax.ShapeDtypeStruct(shape, jnp.float32),
        in_specs=[pl.BlockSpec(memory_space=pltpu.VMEM)] * 2,
        out_specs=pl.BlockSpec(memory_space=pltpu.VMEM),
        scratch_shapes=[pltpu.VMEM((kinds, ladder.shape[1], lanes), jnp.float32)],
        compiler_params=pltpu.CompilerParams(vmem_limit_bytes=room),
    )(ladder, blocks)


def local(amplitudes, fit_out, fit_con, hole_hole):
    norbs = hole_hole.shape[0]
    naux = fit_con.shape[0]
    highs, mids, lots = lax.axis_size("out_hi"), lax.axis_size("out_mid"), lax.axis_size("out_lo")
    lines, cores, occs = lax.axis_size("row"), lax.axis_size("core"), lax.axis_size("occ")
    cons = lines * cores
    cols = amplitudes.shape[2]
    kept = norbs // (cons * occs)
    _, pairs = fit_out.shape
    rows = pairs // cons
    mid, side = lax.axis_index("out_mid"), lax.axis_index("out_lo")
    dress = jnp.eye(norbs, dtype=jnp.float32) - hole_hole

    share = share_of(jnp.transpose(amplitudes, (1, 2, 0)), fit_con, hole_hole, cons * occs)
    share = share.reshape(cons * occs, *share.shape[2:])
    parts = lax.all_to_all(share, plane, 0, 0, tiled=True)
    fitted = jnp.sum(parts, axis=0)
    beyond = lax.ppermute(fitted, "out_mid", [(0, 1), (1, 0)])
    both = jnp.stack([jnp.where(mid == 0, fitted, beyond), jnp.where(mid == 0, beyond, fitted)])
    whole = lax.all_gather(both, ("out_hi", "core"), axis=0)
    whole = whole.reshape(-1, *whole.shape[2:])
    index = jnp.arange(pairs)
    origin = (index // rows % lines * cores + index // (rows * lines)) * rows + index % rows
    chosen = (index[:, None] == origin[None]).astype(jnp.float32)
    mine = jnp.dot(fit_out, chosen, precision=highest)
    other = lax.ppermute(mine, "out_lo", [(0, 1), (1, 0)])
    planes = [jnp.where(side == 0, mine, other), jnp.where(side == 0, other, mine)]
    wide = pairs // cores
    factors = jnp.stack(
        [jnp.concatenate([p[:, c * wide : (c + 1) * wide] for p in planes], axis=1) for c in range(cores)]
    )
    factors = jnp.broadcast_to(factors[None], (lines, *factors.shape))
    factors = lax.all_to_all(factors.reshape(cons, *factors.shape[2:]), con, 0, 0, tiled=True)
    factors = factors.reshape(naux, lots * wide)
    ladder = contract(whole, factors, lots * lines)
    ladder = lax.all_to_all(ladder, pair, 0, 0, tiled=True)
    ladder = ladder.reshape(lots, lines * rows, lanes)
    orders = jnp.transpose(dress.T.reshape(highs, mids, lots, cols, norbs), (2, 0, 1, 3, 4))
    orders = jnp.pad(orders, ((0, 0),) * 4 + ((0, lanes - norbs),))
    orders = orders.reshape(lots, highs, 1, mids, cols, 1, 1, 1, lanes)
    same = jnp.eye(cores, dtype=jnp.float32).reshape(1, 1, cores, 1, 1, 1, cores, 1, 1)
    kind = jnp.eye(kept, dtype=jnp.float32).reshape(1, 1, 1, 1, 1, kept, 1, kept, 1)
    blocks = (orders * same * kind).reshape(lots, lanes, cores * kept * lanes)
    blocks = pieces_of(blocks)
    return finish(ladder, blocks, (rows, cons * kept, norbs))


def solution(mesh):
    shape = dict(mesh.shape)
    out = ("out_hi", "out_mid", "out_lo")
    sizes = (shape["out"] // 4, 2, 2, shape["con"] // 2, 2, shape["occ"])
    finer = Mesh(mesh.devices.reshape(sizes), (*out, *con, "occ"))
    return jax.shard_map(
        local,
        mesh=finer,
        in_specs=(P(con, "occ", out), P(con, out), P(None, con), P()),
        out_specs=P((*out, *con), "occ", None),
        check_vma=False,
    )
```

```python
import jax
import jax.numpy as jnp
from jax import lax
from jax.experimental import pallas as pl
from jax.experimental.pallas import tpu as pltpu
from jax.sharding import Mesh, PartitionSpec as P

highest = lax.Precision.HIGHEST
con = ("row", "core")
plane = ("row", "core", "occ")
pair = ("out_lo", "row")
lanes = 128
room = 16 * 1024 * 1024
steps_out = 4


def dot(a, b):
    return jnp.dot(a, b, precision=highest, preferred_element_type=jnp.float32)


def parted(a):
    high = a.astype(jnp.bfloat16)
    rest = a - high.astype(jnp.float32)
    middle = rest.astype(jnp.bfloat16)
    return high, middle, (rest - middle.astype(jnp.float32)).astype(jnp.bfloat16)


def narrow(a, b, across):
    return lax.dot_general(a, b, (((1,), (across,)), ((), ())), preferred_element_type=jnp.float32)


def thin_dot(a, parts, across):
    high, middle, low = parts
    rows = a[0].shape[0]
    first = narrow(jnp.concatenate(a, axis=0), high, across)
    second = narrow(jnp.concatenate(a[:2], axis=0), middle, across)
    third = narrow(a[0], low, across)
    small = first[2 * rows :] + second[rows:] + third
    return first[:rows] + (first[rows : 2 * rows] + second[:rows] + small)


def lower_rows(shape):
    return lax.broadcasted_iota(jnp.int32, shape, len(shape) - 2) < shape[-2] // 2


def share_kernel(given_ref, lined_ref, hole_ref, share_ref, given, lined, hole, padded, share, arrived, left):
    own, cols, width = given.shape
    norbs = hole.shape[0]
    steps, _, chunk, _ = lined.shape
    blocks = 2 * share.shape[0]
    occs = norbs // own
    kept = norbs // blocks
    copies = [
        pltpu.make_async_copy(given_ref, given, arrived.at[0]),
        pltpu.make_async_copy(hole_ref, hole, arrived.at[1]),
    ]
    for q in range(steps):
        copies.append(pltpu.make_async_copy(lined_ref.at[:, q], lined.at[q], arrived.at[2 + q]))
    for copy in copies:
        copy.start()
    padded[...] = jnp.zeros_like(padded)
    square = (blocks * cols * kept, cols * norbs)
    place = lax.broadcasted_iota(jnp.int32, square, 0)
    index = lax.broadcasted_iota(jnp.int32, square, 1)
    device, inner = place // (cols * kept), place % (cols * kept)
    wanted = (device % occs) * own + (device // occs) * kept + inner % kept + inner // kept * norbs
    chosen = jnp.where(wanted == index, 1.0, 0.0).astype(jnp.bfloat16)
    square = (norbs, norbs)
    unit = lax.broadcasted_iota(jnp.int32, square, 0) == lax.broadcasted_iota(jnp.int32, square, 1)
    first = pl.multiple_of(lax.axis_index("occ") * own, own)
    copies[0].wait()
    for j in range(cols):
        padded[pl.ds(first, own), j * width : (j + 1) * width] = given[:, j, :]
    copies[1].wait()
    dressed = dot(jnp.where(unit, 1.0, 0.0) - hole[...], padded[...])
    dressed = jnp.concatenate([dressed[:, j * width : (j + 1) * width] for j in range(cols)], axis=0)
    picked = narrow(chosen, jnp.concatenate(parted(dressed), axis=1), 0)
    total = tuple(picked[:, k * width : (k + 1) * width].astype(jnp.bfloat16) for k in range(3))
    sends = []
    for q in range(steps):
        copies[2 + q].wait()
        term = thin_dot(total, parted(lined[q].reshape(2 * chunk, width)), 1)
        found = [
            term[:, c * chunk : (c + 1) * chunk].reshape(blocks // 2, 2 * cols * kept, chunk) for c in range(2)
        ]
        lower = lower_rows(found[0].shape)
        turned = [pltpu.roll(part, cols * kept, 1) for part in found]
        lot = pl.ds(q * chunk, chunk)
        share[:, 0, :, q * chunk : (q + 1) * chunk] = jnp.where(lower, found[0], turned[1])
        share[:, 1, :, q * chunk : (q + 1) * chunk] = jnp.where(lower, turned[0], found[1])
        sends.append(
            pltpu.make_async_copy(share.at[:, :, :, lot], share_ref.at[:, :, :, lot], left.at[q])
        )
        sends[-1].start()
    for send in sends:
        send.wait()


def share_of(given, lined, hole, blocks):
    steps = 4
    naux, width = lined.shape
    rows = 2 * given.shape[1] * hole.shape[0] // blocks
    shape = (blocks // 2, 2, rows, naux // 2)
    chunk = naux // 2 // steps
    return pl.pallas_call(
        share_kernel,
        out_shape=jax.ShapeDtypeStruct(shape, jnp.float32),
        in_specs=[pl.BlockSpec(memory_space=pl.ANY)] * 3,
        out_specs=pl.BlockSpec(memory_space=pl.ANY),
        scratch_shapes=[
            pltpu.VMEM(given.shape, jnp.float32),
            pltpu.VMEM((steps, 2, chunk, width), jnp.float32),
            pltpu.VMEM(hole.shape, jnp.float32),
            pltpu.VMEM((hole.shape[0], given.shape[1] * given.shape[2]), jnp.float32),
            pltpu.VMEM(shape, jnp.float32),
            pltpu.SemaphoreType.DMA((2 + steps,)),
            pltpu.SemaphoreType.DMA((steps,)),
        ],
    )(given, lined.reshape(2, steps, chunk, width), hole)


def contract_kernel(fitted_ref, factors_ref, ladder_ref):
    halves, rows, half = fitted_ref.shape
    found = fitted_ref[...].reshape(halves // 2, 2, rows, half)
    even, odd = found[:, 0], found[:, 1]
    lower = lower_rows(even.shape)
    parts = (
        jnp.where(lower, even, pltpu.roll(odd, rows // 2, 1)),
        jnp.where(lower, pltpu.roll(even, rows // 2, 1), odd),
    )
    total = None
    for c in range(2):
        fitted = parted(parts[c].reshape(halves * rows // 2, half))
        term = thin_dot(fitted, parted(factors_ref[c * half : (c + 1) * half, :]), 0)
        total = term if c == 0 else total + term
    ladder_ref[...] = total.T.reshape(ladder_ref.shape)


def contract(fitted, factors, blocks):
    cols, pairs = fitted.shape[0] * fitted.shape[1] // 2, factors.shape[1]
    return pl.pallas_call(
        contract_kernel,
        out_shape=jax.ShapeDtypeStruct((blocks, pairs // blocks, cols), jnp.float32),
        in_specs=[pl.BlockSpec(memory_space=pltpu.VMEM)] * 2,
        out_specs=pl.BlockSpec(memory_space=pltpu.VMEM),
        compiler_params=pltpu.CompilerParams(vmem_limit_bytes=room),
    )(fitted, factors)


def pieces_kernel(blocks_ref, pieces_ref):
    for k, piece in enumerate(parted(blocks_ref[...])):
        pieces_ref[k] = piece


def pieces_of(blocks):
    return pl.pallas_call(
        pieces_kernel,
        out_shape=jax.ShapeDtypeStruct((3, *blocks.shape), jnp.bfloat16),
        in_specs=[pl.BlockSpec(memory_space=pltpu.VMEM)],
        out_specs=pl.BlockSpec(memory_space=pltpu.VMEM),
        compiler_params=pltpu.CompilerParams(vmem_limit_bytes=room),
    )(blocks)


def finish_kernel(ladder_ref, blocks_ref, out_ref, held, result, left):
    lots = blocks_ref.shape[1]
    total = None
    for z in range(lots):
        term = thin_dot(parted(ladder_ref[z]), tuple(blocks_ref[k, z] for k in range(3)), 0)
        total = term if z == 0 else total + term
    kinds = held.shape[0]
    rows, _, norbs = out_ref.shape
    lines = out_ref.shape[1] // kinds
    for s in range(kinds):
        held[s] = total[:, s * lanes : (s + 1) * lanes]
    lot, sends = rows // steps_out, []
    for q in range(steps_out):
        for r in range(q * lot, (q + 1) * lot):
            for s in range(kinds):
                line = held[s, pl.ds(r, lines, stride=rows), :]
                result[r, pl.ds(s, lines, stride=kinds), :] = line[:, :norbs]
        part = pl.ds(q * lot, lot)
        sends.append(pltpu.make_async_copy(result.at[part], out_ref.at[part], left.at[q]))
        sends[-1].start()
    for send in sends:
        send.wait()


def finish(ladder, blocks, shape):
    kinds = blocks.shape[3] // lanes
    return pl.pallas_call(
        finish_kernel,
        out_shape=jax.ShapeDtypeStruct(shape, jnp.float32),
        in_specs=[pl.BlockSpec(memory_space=pltpu.VMEM)] * 2,
        out_specs=pl.BlockSpec(memory_space=pl.ANY),
        scratch_shapes=[
            pltpu.VMEM((kinds, ladder.shape[1], lanes), jnp.float32),
            pltpu.VMEM(shape, jnp.float32),
            pltpu.SemaphoreType.DMA((steps_out,)),
        ],
        compiler_params=pltpu.CompilerParams(vmem_limit_bytes=room),
    )(ladder, blocks)


def local(amplitudes, fit_out, fit_con, hole_hole):
    norbs = hole_hole.shape[0]
    naux = fit_con.shape[0]
    highs, mids, lots = lax.axis_size("out_hi"), lax.axis_size("out_mid"), lax.axis_size("out_lo")
    lines, cores, occs = lax.axis_size("row"), lax.axis_size("core"), lax.axis_size("occ")
    cons = lines * cores
    cols = amplitudes.shape[2]
    kept = norbs // (cons * occs)
    _, pairs = fit_out.shape
    rows = pairs // cons
    mid, side = lax.axis_index("out_mid"), lax.axis_index("out_lo")
    dress = jnp.eye(norbs, dtype=jnp.float32) - hole_hole

    share = share_of(jnp.transpose(amplitudes, (1, 2, 0)), fit_con, hole_hole, cons * occs)
    share = share.reshape(cons * occs, *share.shape[2:])
    parts = lax.all_to_all(share, plane, 0, 0, tiled=True)
    fitted = jnp.sum(parts, axis=0)
    beyond = lax.ppermute(fitted, "out_mid", [(0, 1), (1, 0)])
    both = jnp.stack([jnp.where(mid == 0, fitted, beyond), jnp.where(mid == 0, beyond, fitted)])
    whole = lax.all_gather(both, ("out_hi", "core"), axis=0)
    whole = whole.reshape(-1, *whole.shape[2:])
    index = jnp.arange(pairs)
    origin = (index // rows % lines * cores + index // (rows * lines)) * rows + index % rows
    chosen = (index[:, None] == origin[None]).astype(jnp.float32)
    mine = jnp.dot(fit_out, chosen, precision=highest)
    other = lax.ppermute(mine, "out_lo", [(0, 1), (1, 0)])
    planes = [jnp.where(side == 0, mine, other), jnp.where(side == 0, other, mine)]
    wide = pairs // cores
    factors = jnp.stack(
        [jnp.concatenate([p[:, c * wide : (c + 1) * wide] for p in planes], axis=1) for c in range(cores)]
    )
    factors = jnp.broadcast_to(factors[None], (lines, *factors.shape))
    factors = lax.all_to_all(factors.reshape(cons, *factors.shape[2:]), con, 0, 0, tiled=True)
    factors = factors.reshape(naux, lots * wide)
    ladder = contract(whole, factors, lots * lines)
    ladder = lax.all_to_all(ladder, pair, 0, 0, tiled=True)
    ladder = ladder.reshape(lots, lines * rows, lanes)
    orders = jnp.transpose(dress.T.reshape(highs, mids, lots, cols, norbs), (2, 0, 1, 3, 4))
    orders = jnp.pad(orders, ((0, 0),) * 4 + ((0, lanes - norbs),))
    orders = orders.reshape(lots, highs, 1, mids, cols, 1, 1, 1, lanes)
    same = jnp.eye(cores, dtype=jnp.float32).reshape(1, 1, cores, 1, 1, 1, cores, 1, 1)
    kind = jnp.eye(kept, dtype=jnp.float32).reshape(1, 1, 1, 1, 1, kept, 1, kept, 1)
    blocks = (orders * same * kind).reshape(lots, lanes, cores * kept * lanes)
    blocks = pieces_of(blocks)
    return finish(ladder, blocks, (rows, cons * kept, norbs))


def solution(mesh):
    shape = dict(mesh.shape)
    out = ("out_hi", "out_mid", "out_lo")
    sizes = (shape["out"] // 4, 2, 2, shape["con"] // 2, 2, shape["occ"])
    finer = Mesh(mesh.devices.reshape(sizes), (*out, *con, "occ"))
    return jax.shard_map(
        local,
        mesh=finer,
        in_specs=(P(con, "occ", out), P(con, out), P(None, con), P()),
        out_specs=P((*out, *con), "occ", None),
        check_vma=False,
    )
```
